32 devices in a mesh: comm: 4 (over y, x), wide: 8 (over z, core).
Axes of the slice: x: 2, y: 2, z: 4, core: 2. Of those that a mesh axis runs over, the one named last changes fastest.
Arguments:
- feats: bfloat16 [64, 768, 768], P(('comm', 'wide')), may hold values from -6 to 6
- tiles: bfloat16 [64, 3, 768, 768], P(('comm', 'wide')), may hold values from -0.15625 to 0.15625
- tile_src: int32 [64, 3], P(('comm', 'wide')), may hold values from 0 to 5
- tile_count: int32 [64], P(('comm', 'wide')), may hold values from 1 to 3
- request: int32 [32, 4], P(('comm', 'wide')), may hold values from 0 to 1
- z_old: bfloat16 [64, 768, 1024], P(('comm', 'wide')), may hold values from -6 to 6
- dual: bfloat16 [64, 768, 1024], P(('comm', 'wide')), may hold values from -6 to 6
- target: bfloat16 [64, 768, 1024], P(('comm', 'wide')), may hold values from 0 to 2
- w_rows: bfloat16 [768, 1024], P('wide'), may hold values from -0.21875 to 0.21875
- rho: float32 [1024], replicated, may hold values from 0.3 to 4
- beta: float32 [1024], replicated, may hold values from 0.3 to 4
Outputs:
- new_z: bfloat16 [64, 768, 1024], P(('comm', 'wide'))
- new_dual: bfloat16 [64, 768, 1024], P(('comm', 'wide'))
- weight_grad: float32 [768, 1024], P('wide')
The draws below stay inside these ranges and needn't reach their ends.
Inputs may be any that keep to these rules, and one draw needn't show every extreme that they name: `tile_src`: entries beyond tile_count of a community are not read.
All inputs are finite; a program needn't handle non-finite values.
Results may differ from the reference program's by a relative error of at most 0.0095.
Values may be sent and summed in bfloat16 or wider, within the bound.
A program may use at most 128 MiB of HBM per device.

```python
import math
import jax
import jax.numpy as jnp
from jax import lax

C = 768
F = 768
H = 1024
TILES = 3
COMM_DEV = 2
COMMS = 64
NODES = 49152
N_COMM = 4
N_WIDE = 8
DEVICES = 32


def plant(result, rng, low, high):
    shape = result.shape
    place = [jax.random.randint(jax.random.fold_in(rng, axis), (), 0, shape[axis]) for axis in range(len(shape))]
    result = result.at[tuple(place)].set(low)
    longest = shape.index(max(shape))
    place[longest] = (place[longest] + 1) % shape[longest]
    return result.at[tuple(place)].set(high)


def shard_levels(own_key, shape, pieces, low, largest):
    def one(dim, shards_of):
        draws = jax.random.uniform(jax.random.fold_in(jax.random.fold_in(own_key, 6), dim), (shards_of,), jnp.float32, low / len(pieces), largest / len(pieces))
        return jnp.repeat(jnp.exp(draws), shape[dim] // shards_of).reshape((-1,) + (1,) * (len(shape) - dim - 1))

    factor_of = one(*pieces[0])
    for cut in pieces[1:]:
        factor_of = factor_of * one(*cut)
    return factor_of


def gaussian(key, shape, spread, most, shards=(), kind=jnp.bfloat16):
    values = jax.random.normal(key, shape, jnp.float32) * spread
    if len(shards) > 0:
        values = shard_levels(key, shape, shards, -0.22, 0.18) * values
    return jnp.clip(values, min=-most, max=most).astype(kind)


def setup_inputs(seed: int = 0) -> dict:
    keys = jax.random.split(jax.random.key(seed), 12)
    return {
        "feats": gaussian(keys[0], (COMMS, C, F), 1.0, 6.0, ((0, 32),)),
        "tiles": gaussian(keys[1], (COMMS, TILES, C, C), (C * 2) ** -0.5, 0.15625, ((0, 32),)),
        "tile_src": plant(jax.random.randint(keys[2], (COMMS, TILES), 0, COMM_DEV + N_COMM), jax.random.fold_in(keys[2], 1), 0, (COMM_DEV + N_COMM) - 1).astype(jnp.int32),
        "tile_count": plant(jax.random.randint(keys[3], (COMMS,), 1, TILES + 1), jax.random.fold_in(keys[3], 1), 1, TILES).astype(jnp.int32),
        "request": plant(jax.random.randint(keys[4], (DEVICES, N_COMM), 0, COMM_DEV), jax.random.fold_in(keys[4], 1), 0, COMM_DEV - 1).astype(jnp.int32),
        "z_old": gaussian(keys[5], (COMMS, C, H), 1.0, 6.0, ((0, 32),)),
        "dual": gaussian(keys[6], (COMMS, C, H), 1.0, 6.0, ((0, 32),)),
        "target": jnp.clip(2.0 * jax.random.uniform(keys[7], (COMMS, C, H), jnp.float32) ** shard_levels(keys[7], (COMMS, C, H), ((0, 32),), -0.2, 0.2), 0.0, 2.0).astype(jnp.bfloat16),
        "w_rows": gaussian(keys[8], (F, H), F ** -0.5, 0.21875, ((0, 8),)),
        "rho": jnp.clip(jnp.exp(jax.random.uniform(keys[9], (H,), jnp.float32, math.log(0.3), math.log(4.0))), 0.3, 4.0),
        "beta": jnp.clip(jnp.exp(jax.random.uniform(keys[10], (H,), jnp.float32, math.log(0.3), math.log(4.0))), 0.3, 4.0),
    }


def reference(feats, tiles, tile_src, tile_count, request, z_old, dual, target, w_rows, rho, beta):
    owner = jnp.arange(COMMS, dtype=jnp.int32) // COMM_DEV
    wide_pos = owner % N_WIDE
    slot = jnp.maximum(tile_src - COMM_DEV, 0).astype(jnp.int32)
    peer_dev = slot * N_WIDE + wide_pos[:, None]
    picked = request[owner[:, None], slot]
    remote = peer_dev * COMM_DEV + picked
    local = owner[:, None] * COMM_DEV + tile_src
    source = jnp.where(tile_src < COMM_DEV, local, remote).astype(jnp.int32)
    live = (jnp.arange(TILES, dtype=jnp.int32)[None, :] < tile_count[:, None]).astype(jnp.float32)

    def one(args):
        tile_set, index, keep = args
        blocks = feats[index].astype(jnp.float32) * keep[:, None, None]
        total = jnp.einsum('tij,tjf->if', tile_set.astype(jnp.float32), blocks)
        return total.astype(jnp.bfloat16)
    agg = lax.map(one, (tiles, source, live))
    flat = agg.reshape(-1, F)
    pre = jnp.dot(flat, w_rows, preferred_element_type=jnp.float32).reshape(COMMS, C, H)
    shifted = pre + dual.astype(jnp.float32) / rho
    active = (rho * shifted + beta * target.astype(jnp.float32)) / (rho + beta)
    znew = jnp.where(z_old > 0, active, shifted)
    new_dual = (dual.astype(jnp.float32) + rho * (pre - znew)).astype(jnp.bfloat16)
    grad = jnp.einsum('nf,nh->fh', flat.astype(jnp.float32), new_dual.reshape(-1, H).astype(jnp.float32))
    grad = grad * (1.0 / math.sqrt(NODES))
    return (znew.astype(jnp.bfloat16), new_dual, grad)
```

```python
import functools
import math

import jax
import jax.numpy as jnp
from jax import lax
from jax.experimental import pallas as pl
from jax.experimental.pallas import tpu as pltpu
from jax.sharding import PartitionSpec as P


VMEM_BYTES = 60 * 1024 * 1024


def row_block(nodes):
    for parts in (2, 3, 4, 6):
        if nodes % parts == 0 and (nodes // parts) % 16 == 0:
            return nodes // parts
    return nodes


def step_kernel(received, slots, index_ref, count_ref, *refs):
    own_ref = refs[0]
    peer_refs = refs[1 : 1 + received]
    (tiles_ref, z_ref, dual_ref, target_ref, w_ref, rho_ref, beta_ref) = refs[
        1 + received : 8 + received
    ]
    newz_ref, newdual_ref, grad_ref = refs[8 + received : 11 + received]
    pool, total, gtotal, sems = refs[11 + received :]
    comm = pl.program_id(0)
    part = pl.program_id(1)
    own_count = own_ref.shape[0]
    first = jnp.logical_and(comm == 0, part == 0)
    last = jnp.logical_and(comm == pl.num_programs(0) - 1, part == pl.num_programs(1) - 1)

    @pl.when(first)
    def _():
        copies = [pltpu.make_async_copy(own_ref, pool.at[pl.ds(0, own_count)], sems.at[0])]
        for at, ref in enumerate(peer_refs):
            copies.append(pltpu.make_async_copy(ref, pool.at[own_count + at], sems.at[1 + at]))
        for copy in copies:
            copy.start()
        for copy in copies:
            copy.wait()
        gtotal[...] = jnp.zeros_like(gtotal)

    total[...] = jnp.dot(
        tiles_ref[0, 0], pool[index_ref[comm, 0]], preferred_element_type=jnp.float32
    )
    for slot in range(1, slots):

        @pl.when(slot < count_ref[comm])
        def _():
            total[...] += jnp.dot(
                tiles_ref[0, slot], pool[index_ref[comm, slot]], preferred_element_type=jnp.float32
            )

    agg = total[...].astype(jnp.bfloat16)
    pre = jnp.dot(agg, w_ref[...], preferred_element_type=jnp.float32)
    rho = rho_ref[...]
    beta = beta_ref[...]
    old_dual = dual_ref[0].astype(jnp.float32)
    shifted = pre + old_dual * (1.0 / rho)
    inverse = 1.0 / (rho + beta)
    active = (rho * shifted + beta * target_ref[0].astype(jnp.float32)) * inverse
    znew = jnp.where(z_ref[0].astype(jnp.float32) > 0, active, shifted)
    newz_ref[0] = znew.astype(jnp.bfloat16)
    new_dual = (old_dual + rho * (pre - znew)).astype(jnp.bfloat16)
    newdual_ref[0] = new_dual
    gtotal[...] += lax.dot_general(
        agg, new_dual, (((0,), (0,)), ((), ())), preferred_element_type=jnp.float32
    )

    @pl.when(last)
    def _():
        grad_ref[...] = gtotal[...].astype(jnp.bfloat16)


def step(index, count, own, peers, tiles, z_old, dual, target, w, rho, beta):
    comms, slots, nodes, _ = tiles.shape
    width, hidden = w.shape
    rows = row_block(nodes)
    data = pl.BlockSpec((1, rows, hidden), lambda c, r, *_: (c, r, 0))
    whole = pl.BlockSpec((width, hidden), lambda c, r, *_: (0, 0))
    vector = pl.BlockSpec((1, hidden), lambda c, r, *_: (0, 0))
    anywhere = pl.BlockSpec(memory_space=pl.ANY)
    flops = 2 * comms * nodes * (slots * nodes * width + 2 * width * hidden)
    return pl.pallas_call(
        functools.partial(step_kernel, len(peers), slots),
        grid_spec=pltpu.PrefetchScalarGridSpec(
            num_scalar_prefetch=2,
            grid=(comms, nodes // rows),
            in_specs=[anywhere] * (1 + len(peers))
            + [
                pl.BlockSpec((1, slots, rows, nodes), lambda c, r, *_: (c, 0, r, 0)),
                data,
                data,
                data,
                whole,
                vector,
                vector,
            ],
            out_specs=[data, data, whole],
            scratch_shapes=[
                pltpu.VMEM((own.shape[0] + len(peers), nodes, width), jnp.bfloat16),
                pltpu.VMEM((rows, width), jnp.float32),
                pltpu.VMEM((width, hidden), jnp.float32),
                pltpu.SemaphoreType.DMA((1 + len(peers),)),
            ],
        ),
        out_shape=[
            jax.ShapeDtypeStruct(z_old.shape, jnp.bfloat16),
            jax.ShapeDtypeStruct(dual.shape, jnp.bfloat16),
            jax.ShapeDtypeStruct((width, hidden), jnp.bfloat16),
        ],
        compiler_params=pltpu.CompilerParams(
            dimension_semantics=("arbitrary", "arbitrary"), vmem_limit_bytes=VMEM_BYTES
        ),
        cost_estimate=pl.CostEstimate(flops=flops, bytes_accessed=32 << 20, transcendentals=0),
    )(index, count, own, *peers, tiles, z_old, dual, target, w, rho, beta)


def reduce_kernel(
    n_comm, n_wide, factor, grad_ref, out_ref, got_pair, sums, got_wide, got_comm,
    pair_send, pair_recv, wide_send, wide_recv, comm_send, comm_recv,
):
    half = n_wide // 2
    c = lax.axis_index("comm")
    w = lax.axis_index("wide")
    mine = w // 2
    side = lax.rem(w, 2)
    partner = w + 1 - 2 * side

    def signal(to_c, to_w):
        pl.semaphore_signal(
            pltpu.get_barrier_semaphore(),
            inc=1,
            device_id=(to_c, to_w),
            device_id_type=pl.DeviceIdType.MESH,
        )

    signal(c, partner)
    for off in range(1, half):
        signal(c, lax.rem(mine + off, half) * 2 + side)
    for off in range(1, n_comm):
        signal(lax.rem(c + off, n_comm), w)
    pl.semaphore_wait(pltpu.get_barrier_semaphore(), 1 + (half - 1) + (n_comm - 1))

    def remote(src, dst, send, recv, to_c, to_w):
        return pltpu.make_async_remote_copy(
            src_ref=src,
            dst_ref=dst,
            send_sem=send,
            recv_sem=recv,
            device_id=(to_c, to_w),
            device_id_type=pl.DeviceIdType.MESH,
        )

    order = [lax.rem(mine + off, half) for off in range(1, half)] + [mine]
    pair = []
    for at, j in enumerate(order):
        copy = remote(
            grad_ref.at[2 * j + 1 - side],
            got_pair.at[j],
            pair_send.at[at],
            pair_recv.at[j],
            c,
            partner,
        )
        copy.start()
        pair.append(copy)

    def arrived(dst, recv):
        remote(dst, dst, recv, recv, c, partner).wait_recv()

    wide = []
    for at, j in enumerate(order):
        arrived(got_pair.at[j], pair_recv.at[j])
        value = grad_ref[2 * j + side].astype(jnp.float32) + got_pair[j].astype(jnp.float32)
        if at < half - 1:
            sums[at] = value.astype(jnp.bfloat16)
            copy = remote(
                sums.at[at],
                got_wide.at[mine],
                wide_send.at[at],
                wide_recv.at[mine],
                c,
                j * 2 + side,
            )
            copy.start()
            wide.append(copy)
        else:
            total = value
    for off in range(1, half):
        j = lax.rem(mine + off, half)
        arrived(got_wide.at[j], wide_recv.at[j])
        total = total + got_wide[j].astype(jnp.float32)
    got_comm[c] = total.astype(jnp.bfloat16)
    around = []
    for off in range(1, n_comm):
        copy = remote(
            got_comm.at[c],
            got_comm.at[c],
            comm_send.at[off - 1],
            comm_recv.at[c],
            lax.rem(c + off, n_comm),
            w,
        )
        copy.start()
        around.append(copy)
    for off in range(1, n_comm):
        q = lax.rem(c + off, n_comm)
        arrived(got_comm.at[q], comm_recv.at[q])
    result = got_comm[0].astype(jnp.float32)
    for q in range(1, n_comm):
        result = result + got_comm[q].astype(jnp.float32)
    out_ref[...] = result * factor
    for copy in pair + wide + around:
        copy.wait_send()


def reduce_grad(grad, n_comm, n_wide, factor):
    width, hidden = grad.shape
    rows = width // n_wide
    half = n_wide // 2
    block = (rows, hidden)
    return pl.pallas_call(
        functools.partial(reduce_kernel, n_comm, n_wide, factor),
        out_shape=jax.ShapeDtypeStruct(block, jnp.float32),
        in_specs=[pl.BlockSpec(memory_space=pltpu.VMEM)],
        out_specs=pl.BlockSpec(memory_space=pltpu.VMEM),
        scratch_shapes=[
            pltpu.VMEM((half,) + block, jnp.bfloat16),
            pltpu.VMEM((half,) + block, jnp.bfloat16),
            pltpu.VMEM((half,) + block, jnp.bfloat16),
            pltpu.VMEM((n_comm,) + block, jnp.bfloat16),
            pltpu.SemaphoreType.DMA((half,)),
            pltpu.SemaphoreType.DMA((half,)),
            pltpu.SemaphoreType.DMA((half,)),
            pltpu.SemaphoreType.DMA((half,)),
            pltpu.SemaphoreType.DMA((n_comm,)),
            pltpu.SemaphoreType.DMA((n_comm,)),
        ],
        compiler_params=pltpu.CompilerParams(collective_id=0, has_side_effects=True),
    )(grad.reshape((n_wide,) + block))


def local(feats, tiles, tile_src, tile_count, request, z_old, dual, target, w_rows, rho, beta):
    own_count, nodes, width = feats.shape
    hidden = w_rows.shape[1]
    n_comm = lax.axis_size("comm")
    n_wide = lax.axis_size("wide")
    c = lax.axis_index("comm")
    asked = request[0]
    paired = n_comm & (n_comm - 1) == 0

    def towards(off, q):
        return q ^ off if paired else (q + off) % n_comm

    def arriving(off, q):
        return q ^ off if paired else (q - off) % n_comm

    wants, peers = [], []
    for off in range(1, n_comm):
        ask = lax.dynamic_slice_in_dim(asked, arriving(off, c), 1, 0)
        wants.append(lax.ppermute(ask, "comm", [(q, arriving(off, q)) for q in range(n_comm)]))
    for off in range(1, n_comm):
        block = lax.dynamic_index_in_dim(feats, wants[off - 1][0], 0, keepdims=False)
        peers.append(lax.ppermute(block, "comm", [(q, towards(off, q)) for q in range(n_comm)]))
    weight = lax.all_gather(w_rows, "wide", axis=0, tiled=True)

    member = jnp.maximum(tile_src - own_count, 0)
    offset = c ^ member if paired else (c - member) % n_comm
    self_pick = lax.dynamic_index_in_dim(asked, c, 0, keepdims=False)
    remote = jnp.where(member == c, self_pick, own_count + offset - 1)
    index = jnp.where(tile_src < own_count, tile_src, remote)
    index = jnp.clip(index, 0, own_count + n_comm - 2).astype(jnp.int32)

    new_z, new_dual, grad = step(
        index, tile_count, feats, peers, tiles, z_old, dual, target, weight,
        rho.reshape(1, hidden), beta.reshape(1, hidden),
    )
    factor = 1.0 / math.sqrt(own_count * nodes * n_comm * n_wide)
    return new_z, new_dual, reduce_grad(grad, n_comm, n_wide, factor)


def solution(mesh):
    in_specs = (
        P(("comm", "wide"), None, None),
        P(("comm", "wide"), None, None, None),
        P(("comm", "wide"), None),
        P(("comm", "wide")),
        P(("comm", "wide"), None),
        P(("comm", "wide"), None, None),
        P(("comm", "wide"), None, None),
        P(("comm", "wide"), None, None),
        P("wide", None),
        P(),
        P(),
    )
    out_specs = (P(("comm", "wide"), None, None), P(("comm", "wide"), None, None), P("wide", None))
    return jax.shard_map(local, mesh=mesh, in_specs=in_specs, out_specs=out_specs, check_vma=False)
```

```python
import functools
import math

import jax
import jax.numpy as jnp
from jax import lax
from jax.experimental import pallas as pl
from jax.experimental.pallas import tpu as pltpu
from jax.sharding import PartitionSpec as P


VMEM_BYTES = 60 * 1024 * 1024


def row_block(nodes):
    for parts in (2, 3, 4, 6):
        if nodes % parts == 0 and (nodes // parts) % 16 == 0:
            return nodes // parts
    return nodes


def step_kernel(received, slots, index_ref, count_ref, *refs):
    own_ref = refs[0]
    peer_refs = refs[1 : 1 + received]
    (tiles_ref, z_ref, dual_ref, target_ref, w_ref, rho_ref, beta_ref) = refs[
        1 + received : 8 + received
    ]
    newz_ref, newdual_ref, grad_ref = refs[8 + received : 11 + received]
    pool, total, gtotal, sems = refs[11 + received :]
    comm = pl.program_id(0)
    part = pl.program_id(1)
    own_count = own_ref.shape[0]
    first = jnp.logical_and(comm == 0, part == 0)
    last = jnp.logical_and(comm == pl.num_programs(0) - 1, part == pl.num_programs(1) - 1)

    @pl.when(first)
    def _():
        copies = [pltpu.make_async_copy(own_ref, pool.at[pl.ds(0, own_count)], sems.at[0])]
        for at, ref in enumerate(peer_refs):
            copies.append(pltpu.make_async_copy(ref, pool.at[own_count + at], sems.at[1 + at]))
        for copy in copies:
            copy.start()
        for copy in copies:
            copy.wait()
        gtotal[...] = jnp.zeros_like(gtotal)

    total[...] = jnp.dot(
        tiles_ref[0, 0], pool[index_ref[comm, 0]], preferred_element_type=jnp.float32
    )
    for slot in range(1, slots):

        @pl.when(slot < count_ref[comm])
        def _():
            total[...] += jnp.dot(
                tiles_ref[0, slot], pool[index_ref[comm, slot]], preferred_element_type=jnp.float32
            )

    agg = total[...].astype(jnp.bfloat16)
    pre = jnp.dot(agg, w_ref[...], preferred_element_type=jnp.float32)
    rho = rho_ref[...]
    beta = beta_ref[...]
    old_dual = dual_ref[0].astype(jnp.float32)
    shifted = pre + old_dual * (1.0 / rho)
    inverse = 1.0 / (rho + beta)
    active = (rho * shifted + beta * target_ref[0].astype(jnp.float32)) * inverse
    znew = jnp.where(z_ref[0].astype(jnp.float32) > 0, active, shifted)
    newz_ref[0] = znew.astype(jnp.bfloat16)
    new_dual = (old_dual + rho * (pre - znew)).astype(jnp.bfloat16)
    newdual_ref[0] = new_dual
    gtotal[...] += lax.dot_general(
        agg, new_dual, (((0,), (0,)), ((), ())), preferred_element_type=jnp.float32
    )

    @pl.when(last)
    def _():
        grad_ref[...] = gtotal[...].astype(jnp.bfloat16)


def step(index, count, own, peers, tiles, z_old, dual, target, w, rho, beta):
    comms, slots, nodes, _ = tiles.shape
    width, hidden = w.shape
    rows = row_block(nodes)
    data = pl.BlockSpec((1, rows, hidden), lambda c, r, *_: (c, r, 0))
    whole = pl.BlockSpec((width, hidden), lambda c, r, *_: (0, 0))
    vector = pl.BlockSpec((1, hidden), lambda c, r, *_: (0, 0))
    anywhere = pl.BlockSpec(memory_space=pl.ANY)
    flops = 2 * comms * nodes * (slots * nodes * width + 2 * width * hidden)
    return pl.pallas_call(
        functools.partial(step_kernel, len(peers), slots),
        grid_spec=pltpu.PrefetchScalarGridSpec(
            num_scalar_prefetch=2,
            grid=(comms, nodes // rows),
            in_specs=[anywhere] * (1 + len(peers))
            + [
                pl.BlockSpec((1, slots, rows, nodes), lambda c, r, *_: (c, 0, r, 0)),
                data,
                data,
                data,
                whole,
                vector,
                vector,
            ],
            out_specs=[data, data, whole],
            scratch_shapes=[
                pltpu.VMEM((own.shape[0] + len(peers), nodes, width), jnp.bfloat16),
                pltpu.VMEM((rows, width), jnp.float32),
                pltpu.VMEM((width, hidden), jnp.float32),
                pltpu.SemaphoreType.DMA((1 + len(peers),)),
            ],
        ),
        out_shape=[
            jax.ShapeDtypeStruct(z_old.shape, jnp.bfloat16),
            jax.ShapeDtypeStruct(dual.shape, jnp.bfloat16),
            jax.ShapeDtypeStruct((width, hidden), jnp.bfloat16),
        ],
        compiler_params=pltpu.CompilerParams(
            dimension_semantics=("arbitrary", "arbitrary"), vmem_limit_bytes=VMEM_BYTES
        ),
        cost_estimate=pl.CostEstimate(flops=flops, bytes_accessed=32 << 20, transcendentals=0),
    )(index, count, own, *peers, tiles, z_old, dual, target, w, rho, beta)


def reduce_kernel(
    n_comm, n_wide, factor, grad_ref, out_ref, got_pair, sums, got_comm, parts, got_wide, final,
    pair_send, pair_recv, comm_send, comm_recv, wide_send, wide_recv, final_send, final_recv,
):
    half = n_wide // 2
    columns = sums.shape[-1]
    c = lax.axis_index("comm")
    w = lax.axis_index("wide")
    mine = w // 2
    side = lax.rem(w, 2)
    partner = w + 1 - 2 * side

    def signal(to_c, to_w):
        pl.semaphore_signal(
            pltpu.get_barrier_semaphore(),
            inc=1,
            device_id=(to_c, to_w),
            device_id_type=pl.DeviceIdType.MESH,
        )

    signal(c, partner)
    for off in range(1, half):
        signal(c, lax.rem(mine + off, half) * 2 + side)
    for off in range(1, n_comm):
        signal(lax.rem(c + off, n_comm), w)
    pl.semaphore_wait(pltpu.get_barrier_semaphore(), 1 + (half - 1) + (n_comm - 1))

    def remote(src, dst, send, recv, to_c, to_w):
        return pltpu.make_async_remote_copy(
            src_ref=src,
            dst_ref=dst,
            send_sem=send,
            recv_sem=recv,
            device_id=(to_c, to_w),
            device_id_type=pl.DeviceIdType.MESH,
        )

    def arrived(dst, recv):
        remote(dst, dst, recv, recv, c, partner).wait_recv()

    started = []

    def start(*args):
        copy = remote(*args)
        copy.start()
        started.append(copy)

    order = [lax.rem(mine + off, half) for off in range(1, half)] + [mine]
    for at, j in enumerate(order):
        start(
            grad_ref.at[2 * j + 1 - side], got_pair.at[at], pair_send.at[at], pair_recv.at[at],
            c, partner,
        )
    for at, j in enumerate(order):
        arrived(got_pair.at[at], pair_recv.at[at])
        value = grad_ref[2 * j + side].astype(jnp.float32) + got_pair[at].astype(jnp.float32)
        value = value.astype(jnp.bfloat16)
        for q in range(n_comm):
            sums[q, at] = value[:, q * columns : (q + 1) * columns]
        for off in range(1, n_comm):
            q = lax.rem(c + off, n_comm)
            start(
                sums.at[q, at], got_comm.at[c, at], comm_send.at[off - 1, at],
                comm_recv.at[c, at], q, w,
            )
    for at, j in enumerate(order):
        value = sums[c, at].astype(jnp.float32)
        for off in range(1, n_comm):
            q = lax.rem(c + off, n_comm)
            arrived(got_comm.at[q, at], comm_recv.at[q, at])
            value = value + got_comm[q, at].astype(jnp.float32)
        if at < half - 1:
            parts[at] = value.astype(jnp.bfloat16)
            start(
                parts.at[at], got_wide.at[mine], wide_send.at[at], wide_recv.at[mine],
                c, j * 2 + side,
            )
        else:
            total = value
    for off in range(1, half):
        j = lax.rem(mine + off, half)
        arrived(got_wide.at[j], wide_recv.at[j])
        total = total + got_wide[j].astype(jnp.float32)
    final[c] = total.astype(jnp.bfloat16)
    for off in range(1, n_comm):
        start(
            final.at[c], final.at[c], final_send.at[off - 1], final_recv.at[c],
            lax.rem(c + off, n_comm), w,
        )
    for off in range(1, n_comm):
        q = lax.rem(c + off, n_comm)
        arrived(final.at[q], final_recv.at[q])
    for q in range(n_comm):
        out_ref[:, q * columns : (q + 1) * columns] = final[q].astype(jnp.float32) * factor
    for copy in started:
        copy.wait_send()


def reduce_grad(grad, n_comm, n_wide, factor):
    width, hidden = grad.shape
    rows = width // n_wide
    half = n_wide // 2
    block = (rows, hidden)
    piece = (rows, hidden // n_comm)
    return pl.pallas_call(
        functools.partial(reduce_kernel, n_comm, n_wide, factor),
        out_shape=jax.ShapeDtypeStruct(block, jnp.float32),
        in_specs=[pl.BlockSpec(memory_space=pltpu.VMEM)],
        out_specs=pl.BlockSpec(memory_space=pltpu.VMEM),
        scratch_shapes=[
            pltpu.VMEM((half,) + block, jnp.bfloat16),
            pltpu.VMEM((n_comm, half) + piece, jnp.bfloat16),
            pltpu.VMEM((n_comm, half) + piece, jnp.bfloat16),
            pltpu.VMEM((half,) + piece, jnp.bfloat16),
            pltpu.VMEM((half,) + piece, jnp.bfloat16),
            pltpu.VMEM((n_comm,) + piece, jnp.bfloat16),
            pltpu.SemaphoreType.DMA((half,)),
            pltpu.SemaphoreType.DMA((half,)),
            pltpu.SemaphoreType.DMA((n_comm, half)),
            pltpu.SemaphoreType.DMA((n_comm, half)),
            pltpu.SemaphoreType.DMA((half,)),
            pltpu.SemaphoreType.DMA((half,)),
            pltpu.SemaphoreType.DMA((n_comm,)),
            pltpu.SemaphoreType.DMA((n_comm,)),
        ],
        compiler_params=pltpu.CompilerParams(collective_id=0, has_side_effects=True),
    )(grad.reshape((n_wide,) + block))


def local(feats, tiles, tile_src, tile_count, request, z_old, dual, target, w_rows, rho, beta):
    own_count, nodes, width = feats.shape
    hidden = w_rows.shape[1]
    n_comm = lax.axis_size("comm")
    n_wide = lax.axis_size("wide")
    c = lax.axis_index("comm")
    asked = request[0]
    paired = n_comm & (n_comm - 1) == 0

    def towards(off, q):
        return q ^ off if paired else (q + off) % n_comm

    def arriving(off, q):
        return q ^ off if paired else (q - off) % n_comm

    wants, peers = [], []
    for off in range(1, n_comm):
        ask = lax.dynamic_slice_in_dim(asked, arriving(off, c), 1, 0)
        wants.append(lax.ppermute(ask, "comm", [(q, arriving(off, q)) for q in range(n_comm)]))
    for off in range(1, n_comm):
        block = lax.dynamic_index_in_dim(feats, wants[off - 1][0], 0, keepdims=False)
        peers.append(lax.ppermute(block, "comm", [(q, towards(off, q)) for q in range(n_comm)]))
    weight = lax.all_gather(w_rows, "wide", axis=0, tiled=True)

    member = jnp.maximum(tile_src - own_count, 0)
    offset = c ^ member if paired else (c - member) % n_comm
    self_pick = lax.dynamic_index_in_dim(asked, c, 0, keepdims=False)
    remote = jnp.where(member == c, self_pick, own_count + offset - 1)
    index = jnp.where(tile_src < own_count, tile_src, remote)
    index = jnp.clip(index, 0, own_count + n_comm - 2).astype(jnp.int32)

    new_z, new_dual, grad = step(
        index, tile_count, feats, peers, tiles, z_old, dual, target, weight,
        rho.reshape(1, hidden), beta.reshape(1, hidden),
    )
    factor = 1.0 / math.sqrt(own_count * nodes * n_comm * n_wide)
    return new_z, new_dual, reduce_grad(grad, n_comm, n_wide, factor)


def solution(mesh):
    in_specs = (
        P(("comm", "wide"), None, None),
        P(("comm", "wide"), None, None, None),
        P(("comm", "wide"), None),
        P(("comm", "wide")),
        P(("comm", "wide"), None),
        P(("comm", "wide"), None, None),
        P(("comm", "wide"), None, None),
        P(("comm", "wide"), None, None),
        P("wide", None),
        P(),
        P(),
    )
    out_specs = (P(("comm", "wide"), None, None), P(("comm", "wide"), None, None), P("wide", None))
    return jax.shard_map(local, mesh=mesh, in_specs=in_specs, out_specs=out_specs, check_vma=False)
```
